256 devices in a mesh: tiles: 64 (over z, x, core), slide: 4 (over y).
Axes of the slice: x: 4, y: 4, z: 8, core: 2. Of those that a mesh axis runs over, the one named last changes fastest.
Arguments:
- activations: bfloat16 [4, 64, 64, 64, 128], P('slide', 'tiles'), may hold values from -6 to 6
- cotangent: bfloat16 [4, 64, 32, 32, 256], P('slide', 'tiles'), may hold values from -6 to 6
- weights: bfloat16 [3, 3, 128, 256], replicated, may hold values from -0.1875 to 0.1875
- tile_list: int32 [4, 64], P('slide'), may hold values from -1 to 63, as said below
Outputs:
- features_out: bfloat16 [4, 64, 32, 32, 256], P('slide', 'tiles')
- input_grad: bfloat16 [4, 64, 64, 64, 128], P('slide', 'tiles')
- weight_grad: float32 [3, 3, 128, 256], replicated
The draws below stay inside these ranges and needn't reach their ends.
Inputs may be any that keep to these rules, and one draw needn't show every extreme that they name: `tile_list`: per slide, no grid tile is named twice; tiles that no slot names are background. In every slide each device along tiles holds at least one occupied slot, and all 1 slots of some device are occupied.
All inputs are finite; a program needn't handle non-finite values.
Results may differ from the reference program's by a relative error of at most 0.0014.
Values may be sent and summed in bfloat16 or wider, within the bound.
No kernel may reach another device: no remote copies, remote signals or barrier semaphores. Data moves between devices by JAX's collectives and lax.ppermute only.
A program may use at most 64 MiB of HBM per device.

```python
import math
import jax
import jax.numpy as jnp
from jax import lax

CIN = 128
COUT = 256
TILE = 64
GW = 8
TPD = 1
SLOTS = 64
GH = 8
SLIDES = 4


def draw_tile_list(key, part):

    def one_slide(slide_key):
        key_occ, key_off, key_perm, key_full, key_pick = jax.random.split(slide_key, 5)
        grid_count = GH * GW
        devices_here = SLOTS // TPD
        run_length = devices_here + TPD - 1
        tile_ids = jnp.arange(grid_count, dtype=jnp.int32)
        occupied = jax.random.randint(key_occ, (grid_count,), 0, 5) < 3
        offset = jax.random.randint(key_off, (), 0, grid_count - run_length + 1)
        occupied = occupied | (tile_ids >= offset) & (tile_ids < offset + run_length)
        number = jnp.sum(occupied.astype(jnp.int32))
        ranked = jnp.argsort(jnp.where(occupied, tile_ids, grid_count + tile_ids)).astype(jnp.int32)
        tile_at = jnp.where(tile_ids < number, ranked, -1).astype(jnp.int32)
        slot_ids = jnp.arange(SLOTS, dtype=jnp.int32)
        shuffled = jax.random.permutation(key_perm, SLOTS).astype(jnp.int32)
        full_device = jax.random.randint(key_full, (), 0, devices_here)
        first_pick = jax.random.randint(key_pick, (devices_here,), 0, TPD)
        chosen_slot = slot_ids % TPD == jnp.take(first_pick, slot_ids // TPD)
        scores = shuffled + jnp.where(chosen_slot, -SLOTS, 0).astype(jnp.int32)
        scores = scores + jnp.where(slot_ids // TPD == full_device, -2 * SLOTS, 0).astype(jnp.int32)
        order = jnp.argsort(scores).astype(jnp.int32)
        return jnp.zeros((SLOTS,), jnp.int32).at[order].set(tile_at)
    slide_keys = jax.random.split(key, SLIDES)
    return jax.vmap(one_slide)(slide_keys)


def shard_levels(own_key, shape, cuts, smallest, high):
    level = 1.0
    for position, parts in cuts:
        heights = jax.random.uniform(jax.random.fold_in(jax.random.fold_in(own_key, 6), position), (parts,), jnp.float32, smallest / len(cuts), high / len(cuts))
        level = level * jnp.repeat(jnp.exp(heights), shape[position] // parts).reshape((-1,) + (1,) * (len(shape) - 1 - position))
    return level


def centred(own_key, shape, scale, reach, shards=(), held_as=jnp.bfloat16):
    values = scale * jax.random.normal(own_key, shape, jnp.float32)
    if shards:
        values = values * shard_levels(own_key, shape, shards, -0.22, 0.18)
    return jnp.clip(values, -reach, reach).astype(held_as)


def setup_inputs(seed: int = 0) -> dict:
    keys = jax.random.split(jax.random.key(seed), 5)
    activations = centred(keys[0], (SLIDES, SLOTS, TILE, TILE, CIN), 1.0, 6.0, ((0, 4), (1, 64)))
    cotangent = centred(keys[1], (SLIDES, SLOTS, TILE // 2, TILE // 2, COUT), 1.0, 6.0, ((0, 4), (1, 64)))
    weights = centred(keys[2], (3, 3, CIN, COUT), (9 * CIN) ** -0.5, 0.1875)
    tile_list = draw_tile_list(jax.random.fold_in(keys[4], 71), 0)
    return dict(activations=activations, cotangent=cotangent, weights=weights, tile_list=tile_list)


DIRECTIONS = ((-1, 0), (0, -1), (-1, -1), (1, 0), (0, 1), (1, 1))

def find_slots(listing):
    grid_count = GH * GW
    live_here = listing >= 0
    safe_tiles = jnp.where(live_here, listing, grid_count)
    holder = jnp.full((grid_count + 1,), -1, jnp.int32).at[safe_tiles].set(jnp.arange(SLOTS, dtype=jnp.int32))
    tile_row = jnp.where(live_here, listing // GW, 0)
    tile_col = jnp.where(live_here, listing % GW, 0)
    found_all = []
    for row_step, col_step in DIRECTIONS:
        new_row = tile_row + row_step
        new_col = tile_col + col_step
        inside = live_here & (new_row >= 0) & (new_row < GH) & (new_col >= 0) & (new_col < GW)
        target = jnp.where(inside, new_row * GW + new_col, grid_count).astype(jnp.int32)
        found_all.append(jnp.where(inside, holder[target], -1).astype(jnp.int32))
    return found_all

def pick_rows(source_rows, slot_index):
    chosen = jnp.take(source_rows, jnp.maximum(slot_index, 0).astype(jnp.int32), axis=0)
    keep_mask = (slot_index >= 0).astype(source_rows.dtype)
    return chosen * keep_mask.reshape(keep_mask.shape + (1,) * (chosen.ndim - 1))

def convolve(padded, kernel):
    return lax.conv_general_dilated(padded, kernel, (2, 2), 'VALID', dimension_numbers=('NHWC', 'HWIO', 'NHWC'), precision=lax.Precision.HIGHEST)

def reference(activations, cotangent, weights, tile_list):
    weight_full = weights.astype(jnp.float32)

    def one_slide(packed):
        slide_acts, slide_cots, listing = packed
        tile_above, beside, corner_up, tile_below, right_side, corner_down = find_slots(listing)
        live_f = (listing >= 0).astype(jnp.float32)[:, None, None, None]
        inputs = slide_acts.astype(jnp.float32)
        from_above = pick_rows(inputs[:, TILE - 1], tile_above)
        from_left = pick_rows(inputs[:, :, TILE - 1], beside)
        from_diag = pick_rows(inputs[:, TILE - 1, TILE - 1], corner_up)
        top_line = jnp.concatenate([from_diag[:, None], from_above], axis=1)
        lower_rows = jnp.concatenate([from_left[:, :, None], inputs], axis=2)
        padded = jnp.concatenate([top_line[:, None], lower_rows], axis=1)
        result, backward = jax.vjp(convolve, padded, weight_full)
        features = (result * live_f).astype(jnp.bfloat16)
        spread, weight_part = backward(slide_cots.astype(jnp.float32) * live_f)
        top_terms = spread[:, 0]
        left_terms = spread[:, 1:, 0]
        inner_grad = spread[:, 1:, 1:]
        inner_grad = inner_grad.at[:, TILE - 1].add(pick_rows(top_terms[:, 1:], tile_below))
        inner_grad = inner_grad.at[:, :, TILE - 1].add(pick_rows(left_terms, right_side))
        inner_grad = inner_grad.at[:, TILE - 1, TILE - 1].add(pick_rows(top_terms[:, 0], corner_down))
        grads = (inner_grad * live_f).astype(jnp.bfloat16)
        return (features, grads, weight_part)
    features_out, input_grad, weight_parts = lax.map(one_slide, (activations, cotangent, tile_list))
    grad_scale = 1.0 / math.sqrt(SLIDES * SLOTS * (TILE // 2) * (TILE // 2))
    weight_grad = lax.optimization_barrier(jnp.sum(weight_parts, axis=0)) * grad_scale
    return (features_out, input_grad, weight_grad)
```

```python
import functools
import math

import jax
import jax.numpy as jnp
from jax import lax
from jax.experimental import pallas as pl
from jax.experimental.pallas import tpu as pltpu
from jax.sharding import PartitionSpec as P

GW = 8
BF = jnp.bfloat16
F32 = jnp.float32


def vmem_specs(count):
    return [pl.BlockSpec(memory_space=pltpu.VMEM)] * count


def halo_matrices(listing, me, grid_rows):
    row, col = listing // GW, listing % GW
    live = listing >= 0

    def chosen(row_step, col_step):
        new_row, new_col = row + row_step, col + col_step
        inside = live & (new_row >= 0) & (new_row < grid_rows) & (new_col >= 0) & (new_col < GW)
        target = jnp.where(inside, new_row * GW + new_col, -2)
        return listing[None, :] == target[:, None]

    half = listing.shape[0] // 2
    by_row = me < half
    act = jnp.where(by_row, chosen(-1, 0), chosen(0, -1))
    cot = jnp.where(by_row, chosen(1, 0), chosen(0, 1))
    diag = chosen(-1, -1)
    below_right = chosen(1, 1)
    before = jnp.where(me == 0, diag, act & (me != half))
    return jnp.stack([before, act, cot, diag, below_right]).astype(BF)


def pack_kernel(row_ref, col_ref, crow_ref, ccol_ref, out_ref, tall, line, both):
    def fill(base, values, cot_values):
        line[8:72, :] = values
        line[7:8, :] = values[63:64, :]
        for slot in range(3):
            both[pl.ds(base * 8 + slot, 32, stride=8), :] = line[pl.ds(7 + slot, 32, stride=2), :]
        both[pl.ds(base * 8 + 3, 32, stride=8), :] = cot_values[:, 0:128]
        both[pl.ds(base * 8 + 4, 32, stride=8), :] = cot_values[:, 128:256]

    both[...] = jnp.zeros_like(both)
    fill(0, row_ref[0].astype(F32), crow_ref[0].astype(F32))
    tall[...] = col_ref[...].astype(F32).reshape(512, 128)
    values = tall[pl.ds(7, 64, stride=8), :]
    tall[0:256, :] = ccol_ref[:, :, 0:128].astype(F32).reshape(256, 128)
    tall[256:512, :] = ccol_ref[:, :, 128:256].astype(F32).reshape(256, 128)
    low = tall[pl.ds(0, 32, stride=8), :]
    high = tall[pl.ds(256, 32, stride=8), :]
    fill(32, values, jnp.concatenate([low, high], axis=1))
    out_ref[...] = both[...].reshape(64, 8, 128).astype(BF)


def pack_edges(act, cot):
    return pl.pallas_call(
        pack_kernel,
        grid=(1,),
        in_specs=[
            pl.BlockSpec((1, 64, 128), lambda i: (63, 0, 0)),
            pl.BlockSpec((64, 8, 128), lambda i: (0, 7, 0)),
            pl.BlockSpec((1, 32, 256), lambda i: (0, 0, 0)),
            pl.BlockSpec((32, 8, 256), lambda i: (0, 0, 0)),
        ],
        out_specs=pl.BlockSpec((64, 8, 128), lambda i: (0, 0, 0)),
        out_shape=jax.ShapeDtypeStruct((64, 8, 128), BF),
        scratch_shapes=[
            pltpu.VMEM((512, 128), F32),
            pltpu.VMEM((72, 128), F32),
            pltpu.VMEM((512, 128), F32),
        ],
        name="pack_edges",
    )(act, act, cot, cot)


def fill_patches(act_ref, even, odd, wide, left):
    def one_row(i, carry):
        for parity in range(2):
            p = 2 * i + parity
            wide[parity, 8:72, :] = act_ref[p].astype(F32)
            if left is not None:
                wide[parity, 7:8, :] = left[parity, pl.ds(i, 1), :]
        for parity in range(2):
            dest = odd if parity == 0 else even
            start = pl.multiple_of((i + parity) * 32, 32)
            for b in range(3):
                dest[pl.ds(start, 32), b * 128 : (b + 1) * 128] = wide[
                    parity, pl.ds(7 + b, 32, stride=2), :
                ].astype(BF)
        return carry

    lax.fori_loop(0, 32, one_row, 0, unroll=4)


def weight_kernel(live_ref, act_ref, cot_ref, out_ref, even, odd, wide):
    even[0:32, :] = jnp.zeros((32, 384), BF)
    for parity in range(2):
        wide[parity, 0:8, :] = jnp.zeros((8, 128), F32)
    fill_patches(act_ref, even, odd, wide, None)
    live = live_ref[0].astype(F32).astype(BF)
    cot = cot_ref[...].reshape(1024, 256) * live
    for a, rows in enumerate((even[0:1024, :], odd[...], even[32:1056, :])):
        out_ref[:, a * 384 : (a + 1) * 384] = lax.dot_general(
            cot, rows, (((0,), (0,)), ((), ())), preferred_element_type=F32
        )


def interior_weights(live, act, cot):
    return pl.pallas_call(
        weight_kernel,
        in_specs=[pl.BlockSpec(memory_space=pltpu.SMEM)] + vmem_specs(2),
        out_specs=vmem_specs(1)[0],
        out_shape=jax.ShapeDtypeStruct((256, 1152), F32),
        scratch_shapes=[
            pltpu.VMEM((1056, 384), BF),
            pltpu.VMEM((1024, 384), BF),
            pltpu.VMEM((2, 72, 128), F32),
        ],
        cost_estimate=pl.CostEstimate(
            flops=2 * 1024 * 1152 * 256, bytes_accessed=3 << 20, transcendentals=0
        ),
        name="interior_weights",
    )(live, act, cot)


def turn_kernel(role_ref, pieces_ref, select_ref, grad_ref, back_ref, out_ref, tall):
    tall[...] = pieces_ref[...].astype(F32).reshape(512, 128)
    slots = [tall[pl.ds(slot, 64, stride=8), :].astype(BF) for slot in range(5)]
    cot = jnp.concatenate(slots[3:5], axis=1)

    def pick(which, values):
        return jnp.dot(select_ref[which], values, preferred_element_type=F32)

    before, first, second = pick(0, slots[0]), pick(1, slots[1]), pick(1, slots[2])
    returned = pick(2, cot)
    corner = pick(4, cot)
    tall[pl.ds(0, 64, stride=8), :] = first
    tall[pl.ds(1, 64, stride=8), :] = second
    tall[pl.ds(2, 64, stride=8), :] = returned[:, 0:128]
    tall[pl.ds(3, 64, stride=8), :] = returned[:, 128:256]
    tall[pl.ds(4, 64, stride=8), :] = pick(3, slots[0])
    tall[pl.ds(5, 64, stride=8), :] = corner[:, 0:128]
    tall[pl.ds(6, 64, stride=8), :] = corner[:, 128:256]
    tall[pl.ds(7, 64, stride=8), :] = corner[:, 0:128]
    back_ref[...] = tall[...].reshape(64, 8, 128).astype(BF)
    out_ref[...] = grad_ref[...]
    step = role_ref[0]
    for b, values in enumerate((before, first, second)):
        terms = lax.dot_general(
            cot, values.astype(BF), (((0,), (0,)), ((), ())), preferred_element_type=F32
        )
        at = pl.ds(pl.multiple_of(b * step * 128, 128), 128)
        out_ref[:, at] = out_ref[:, at] + terms


def turn_edges(step, pieces, select, grad):
    return pl.pallas_call(
        turn_kernel,
        in_specs=[pl.BlockSpec(memory_space=pltpu.SMEM)] + vmem_specs(3),
        out_specs=vmem_specs(2),
        out_shape=[
            jax.ShapeDtypeStruct((64, 8, 128), BF),
            jax.ShapeDtypeStruct((256, 1152), F32),
        ],
        scratch_shapes=[pltpu.VMEM((512, 128), F32)],
        name="turn_edges",
    )(step, pieces, select, grad)


def tile_kernel(
    live_ref, act_ref, cot_ref, weight_ref, halo_ref, feat_ref, grad_ref,
    even, odd, wide, tall, left, line, shift, around, mix, lines,
):
    live = live_ref[0].astype(F32)
    tall[...] = halo_ref[...].astype(F32).reshape(512, 128)
    first = tall[pl.ds(0, 32, stride=8), :]
    second = tall[pl.ds(1, 32, stride=8), :]
    line[8:40, :] = second
    line[7:8, :] = tall[4:5, :]
    even[0:32, 0:128] = line[7:39, :].astype(BF)
    even[0:32, 128:256] = first.astype(BF)
    even[0:32, 256:384] = second.astype(BF)
    left[0] = tall[pl.ds(256, 32, stride=8), :]
    left[1] = tall[pl.ds(257, 32, stride=8), :]
    fill_patches(act_ref, even, odd, wide, left)
    result = jnp.dot(even[0:1024, :], weight_ref[0:384, :], preferred_element_type=F32)
    result += jnp.dot(odd[...], weight_ref[384:768, :], preferred_element_type=F32)
    result += jnp.dot(even[32:1056, :], weight_ref[768:1152, :], preferred_element_type=F32)
    feat_ref[...] = (result * live).astype(BF).reshape(32, 32, 256)

    right = jnp.concatenate(
        [tall[pl.ds(258, 32, stride=8), :], tall[pl.ds(259, 32, stride=8), :]], axis=1
    )
    around[0:32, :] = right
    around[32:33, 0:128] = tall[5:6, :]
    around[32:33, 128:256] = tall[6:7, :]
    below = jnp.concatenate(
        [tall[pl.ds(2, 32, stride=8), :], tall[pl.ds(3, 32, stride=8), :]], axis=1
    )

    def place(i, values):
        shift[0:32, :] = values
        shift[32:33, :] = around[pl.ds(i, 1), :]
        at = pl.ds(pl.multiple_of(i * 32, 32), 32)
        mix[at, 0:256] = values.astype(BF)
        mix[at, 256:512] = shift[1:33, :].astype(BF)

    def one_row(i, carry):
        place(i, cot_ref[i].astype(F32))
        return carry

    lax.fori_loop(0, 32, one_row, 0, unroll=4)
    place(32, below)

    def tap(a, b):
        at = (3 * a + b) * 128
        return weight_ref[at : at + 128, :]

    none = jnp.zeros((128, 256), BF)

    def block(even_taps, odd_taps):
        return jnp.concatenate(
            [jnp.concatenate(even_taps, axis=1), jnp.concatenate(odd_taps, axis=1)], axis=0
        )

    def back(rows, matrix):
        return lax.dot_general(
            rows, matrix, (((1,), (1,)), ((), ())), preferred_element_type=F32
        )

    here, after = mix[0:1024, :], mix[32:1056, :]
    lines[0] = back(here, block([tap(1, 1), none], [tap(1, 2), tap(1, 0)])) * live
    lines[1] = (
        back(here, block([tap(2, 1), none], [tap(2, 2), tap(2, 0)]))
        + back(after, block([tap(0, 1), none], [tap(0, 2), tap(0, 0)]))
    ) * live

    def weave(i, carry):
        at = pl.ds(pl.multiple_of(i * 32, 32), 32)
        for parity in range(2):
            for side in range(2):
                wide[parity, pl.ds(8 + side, 32, stride=2), :] = lines[
                    parity, at, side * 128 : (side + 1) * 128
                ]
            grad_ref[2 * i + parity] = wide[parity, 8:72, :].astype(BF)
        return carry

    lax.fori_loop(0, 32, weave, 0, unroll=4)


def tile_terms(live, act, cot, weight_matrix, halo):
    return pl.pallas_call(
        tile_kernel,
        in_specs=[pl.BlockSpec(memory_space=pltpu.SMEM)] + vmem_specs(4),
        out_specs=vmem_specs(2),
        out_shape=[
            jax.ShapeDtypeStruct((32, 32, 256), BF),
            jax.ShapeDtypeStruct((64, 64, 128), BF),
        ],
        scratch_shapes=[
            pltpu.VMEM((1056, 384), BF),
            pltpu.VMEM((1024, 384), BF),
            pltpu.VMEM((2, 72, 128), F32),
            pltpu.VMEM((512, 128), F32),
            pltpu.VMEM((2, 32, 128), F32),
            pltpu.VMEM((40, 128), F32),
            pltpu.VMEM((40, 256), F32),
            pltpu.VMEM((40, 256), F32),
            pltpu.VMEM((1056, 512), BF),
            pltpu.VMEM((2, 1024, 256), F32),
        ],
        cost_estimate=pl.CostEstimate(
            flops=5 * 1024 * 1152 * 256, bytes_accessed=4 << 20, transcendentals=0
        ),
        name="tile_terms",
    )(live, act, cot, weight_matrix, halo)


def shards(activations, cotangent, weights, tile_list):
    act, cot = activations[0, 0], cotangent[0, 0]
    slots = lax.axis_size("tiles")
    slides = lax.axis_size("slide")
    half_side = cot.shape[0]
    listing = tile_list[0]
    me = lax.axis_index("tiles")
    live = (lax.dynamic_slice_in_dim(listing, me, 1) >= 0).astype(jnp.int32)
    step = jnp.where(me < slots // 2, 1, 3).astype(jnp.int32).reshape(1)
    select = halo_matrices(listing, me, slots // GW)
    weight_matrix = weights.reshape(-1, weights.shape[3])

    pieces = lax.all_to_all(pack_edges(act, cot), "tiles", 0, 0, tiled=True)
    inner = interior_weights(live, act, cot)
    back, local_grad = turn_edges(step, pieces, select, inner)
    halo = lax.all_to_all(back, "tiles", 0, 0, tiled=True)
    features_out, input_grad = tile_terms(live, act, cot, weight_matrix, halo)

    own = lax.axis_index("slide")
    quarters = local_grad.reshape(slides, slots, -1)

    def quarter(which):
        return lax.dynamic_index_in_dim(quarters, which % slides, 0, keepdims=False)

    total = quarter(own)
    for hop in range(1, slides):
        total = total + lax.ppermute(
            quarter(own + hop), "slide", [(i, (i + hop) % slides) for i in range(slides)]
        )
    rows = lax.all_to_all(total[:, None, :], "tiles", 0, 0, tiled=True)
    grad_scale = 1.0 / math.sqrt(slides * slots * half_side * half_side)
    row = jnp.sum(rows, axis=0, keepdims=True) * grad_scale
    spread = lax.all_to_all(jnp.broadcast_to(row, rows.shape), "tiles", 0, 0, tiled=True)
    mine = spread[:, 0, :]
    placed = [mine]
    for hop in range(1, slides):
        placed.append(
            lax.ppermute(mine, "slide", [(i, (i + hop) % slides) for i in range(slides)])
        )
    stacked = jnp.stack(placed)
    order = (own - jnp.arange(slides)) % slides
    ordered = jnp.take(stacked, order, axis=0)
    weight_grad = ordered.reshape(slides * slots, -1).T.reshape(weights.shape)
    return (features_out[None, None], input_grad[None, None], weight_grad)


def solution(mesh):
    placed = (
        P("slide", "tiles", None, None, None),
        P("slide", "tiles", None, None, None),
        P(),
        P("slide", None),
    )
    return jax.shard_map(
        shards,
        mesh=mesh,
        in_specs=placed,
        out_specs=(
            P("slide", "tiles", None, None, None),
            P("slide", "tiles", None, None, None),
            P(),
        ),
        check_vma=False,
    )
```

```python
import math

import jax
import jax.numpy as jnp
from jax import lax
from jax.experimental import pallas as pl
from jax.experimental.pallas import tpu as pltpu
from jax.sharding import PartitionSpec as P


GW = 8
BF = jnp.bfloat16
F32 = jnp.float32


def grant(mebibytes):
    return pltpu.CompilerParams(vmem_limit_bytes=mebibytes << 20)


def vmem_specs(count):
    return [pl.BlockSpec(memory_space=pltpu.VMEM)] * count


def halo_matrices(listing, me, grid_rows):
    row, col = listing // GW, listing % GW
    live = listing >= 0

    def chosen(row_step, col_step):
        new_row, new_col = row + row_step, col + col_step
        inside = live & (new_row >= 0) & (new_row < grid_rows) & (new_col >= 0) & (new_col < GW)
        target = jnp.where(inside, new_row * GW + new_col, -2)
        return listing[None, :] == target[:, None]

    half = listing.shape[0] // 2
    by_row = me < half
    act = jnp.where(by_row, chosen(-1, 0), chosen(0, -1))
    cot = jnp.where(by_row, chosen(1, 0), chosen(0, 1))
    diag = chosen(-1, -1)
    below_right = chosen(1, 1)
    before = jnp.where(me == 0, diag, act & (me != half))
    return jnp.stack([before, act, cot, diag, below_right]).astype(BF)


def pack_kernel(
    act_ref, cot_ref, out_ref, row_buf, col_buf, crow_buf, ccol_buf, sems, tall, line, both
):
    copies = [
        pltpu.make_async_copy(act_ref.at[63], row_buf, sems.at[0]),
        pltpu.make_async_copy(act_ref.at[:, 56:64, :], col_buf, sems.at[1]),
        pltpu.make_async_copy(cot_ref.at[0], crow_buf, sems.at[2]),
        pltpu.make_async_copy(cot_ref.at[:, 0:8, :], ccol_buf, sems.at[3]),
    ]
    for copy in copies:
        copy.start()

    def fill(base, values, cot_values):
        line[8:72, :] = values
        line[7:8, :] = values[63:64, :]
        for slot in range(3):
            both[pl.ds(base * 8 + slot, 32, stride=8), :] = line[pl.ds(7 + slot, 32, stride=2), :]
        both[pl.ds(base * 8 + 3, 32, stride=8), :] = cot_values[:, 0:128]
        both[pl.ds(base * 8 + 4, 32, stride=8), :] = cot_values[:, 128:256]

    both[...] = jnp.zeros_like(both)
    for copy in copies:
        copy.wait()
    fill(0, row_buf[...].astype(F32), crow_buf[...].astype(F32))
    tall[...] = col_buf[...].astype(F32).reshape(512, 128)
    values = tall[pl.ds(7, 64, stride=8), :]
    tall[0:256, :] = ccol_buf[:, :, 0:128].astype(F32).reshape(256, 128)
    tall[256:512, :] = ccol_buf[:, :, 128:256].astype(F32).reshape(256, 128)
    low = tall[pl.ds(0, 32, stride=8), :]
    high = tall[pl.ds(256, 32, stride=8), :]
    fill(32, values, jnp.concatenate([low, high], axis=1))
    out_ref[...] = both[...].reshape(64, 8, 128).astype(BF)


def pack_edges(act, cot):
    return pl.pallas_call(
        pack_kernel,
        in_specs=[pl.BlockSpec(memory_space=pltpu.HBM)] * 2,
        out_specs=vmem_specs(1)[0],
        out_shape=jax.ShapeDtypeStruct((64, 8, 128), BF),
        scratch_shapes=[
            pltpu.VMEM((64, 128), BF),
            pltpu.VMEM((64, 8, 128), BF),
            pltpu.VMEM((32, 256), BF),
            pltpu.VMEM((32, 8, 256), BF),
            pltpu.SemaphoreType.DMA((4,)),
            pltpu.VMEM((512, 128), F32),
            pltpu.VMEM((72, 128), F32),
            pltpu.VMEM((512, 128), F32),
        ],
        name="pack_edges",
    )(act, cot)


def fill_patches(act_ref, even, odd, wide, left):
    def one_row(i, carry):
        for parity in range(2):
            p = 2 * i + parity
            wide[parity, 8:72, :] = act_ref[p].astype(F32)
            if left is not None:
                wide[parity, 7:8, :] = left[parity, pl.ds(i, 1), :]
        for parity in range(2):
            dest = odd if parity == 0 else even
            start = pl.multiple_of((i + parity) * 32, 32)
            for b in range(3):
                dest[pl.ds(start, 32), b * 128 : (b + 1) * 128] = wide[
                    parity, pl.ds(7 + b, 32, stride=2), :
                ].astype(BF)
        return carry

    lax.fori_loop(0, 32, one_row, 0, unroll=4)


def weight_kernel(live_ref, act_ref, cot_ref, out_ref, even, odd, wide):
    even[0:32, :] = jnp.zeros((32, 384), BF)
    for parity in range(2):
        wide[parity, 0:8, :] = jnp.zeros((8, 128), F32)
    fill_patches(act_ref, even, odd, wide, None)
    live = live_ref[0].astype(F32).astype(BF)
    cot = cot_ref[...].reshape(1024, 256) * live
    for a, rows in enumerate((even[0:1024, :], odd[...], even[32:1056, :])):
        out_ref[a * 384 : (a + 1) * 384, :] = lax.dot_general(
            rows, cot, (((0,), (0,)), ((), ())), preferred_element_type=F32
        )


def interior_weights(live, act, cot):
    return pl.pallas_call(
        weight_kernel,
        in_specs=[pl.BlockSpec(memory_space=pltpu.SMEM)] + vmem_specs(2),
        out_specs=vmem_specs(1)[0],
        out_shape=jax.ShapeDtypeStruct((1152, 256), F32),
        scratch_shapes=[
            pltpu.VMEM((1056, 384), BF),
            pltpu.VMEM((1024, 384), BF),
            pltpu.VMEM((2, 72, 128), F32),
        ],
        cost_estimate=pl.CostEstimate(
            flops=2 * 1024 * 1152 * 256, bytes_accessed=3 << 20, transcendentals=0
        ),
        compiler_params=grant(12),
        name="interior_weights",
    )(live, act, cot)


def turn_kernel(
    place_ref, pieces_ref, select_ref, grad_ref, back_ref, keep_ref, send_ref, tall
):
    tall[...] = pieces_ref[...].astype(F32).reshape(512, 128)
    slots = [tall[pl.ds(slot, 64, stride=8), :].astype(BF) for slot in range(5)]
    cot = jnp.concatenate(slots[3:5], axis=1)

    def pick(which, values):
        return jnp.dot(select_ref[which], values, preferred_element_type=F32)

    before, first, second = pick(0, slots[0]), pick(1, slots[1]), pick(1, slots[2])
    returned = pick(2, cot)
    corner = pick(4, cot)
    tall[pl.ds(0, 64, stride=8), :] = first
    tall[pl.ds(1, 64, stride=8), :] = second
    tall[pl.ds(2, 64, stride=8), :] = returned[:, 0:128]
    tall[pl.ds(3, 64, stride=8), :] = returned[:, 128:256]
    tall[pl.ds(4, 64, stride=8), :] = pick(3, slots[0])
    tall[pl.ds(5, 64, stride=8), :] = corner[:, 0:128]
    tall[pl.ds(6, 64, stride=8), :] = corner[:, 128:256]
    tall[pl.ds(7, 64, stride=8), :] = corner[:, 0:128]
    back_ref[...] = tall[...].reshape(64, 8, 128).astype(BF)
    step, core = place_ref[0], place_ref[1]

    def split(at, values):
        low, high = values[:, 0:128], values[:, 128:256]
        first_core = core == 0
        keep_ref[at, :] = jnp.where(first_core, low, high)
        send_ref[at, :] = jnp.where(first_core, high, low)

    split(pl.ds(0, 1152), grad_ref[...])
    for b, values in enumerate((before, first, second)):
        at = pl.ds(pl.multiple_of(b * step * 128, 128), 128)
        terms = lax.dot_general(
            values.astype(BF), cot, (((0,), (0,)), ((), ())), preferred_element_type=F32
        )
        split(at, grad_ref[at, :] + terms)


def turn_edges(place, pieces, select, grad):
    return pl.pallas_call(
        turn_kernel,
        in_specs=[pl.BlockSpec(memory_space=pltpu.SMEM)] + vmem_specs(3),
        out_specs=vmem_specs(3),
        out_shape=[
            jax.ShapeDtypeStruct((64, 8, 128), BF),
            jax.ShapeDtypeStruct((1152, 128), F32),
            jax.ShapeDtypeStruct((1152, 128), F32),
        ],
        scratch_shapes=[pltpu.VMEM((512, 128), F32)],
        compiler_params=grant(10),
        name="turn_edges",
    )(place, pieces, select, grad)


def sum_and_cut(place, which, parts):
    rows = parts[0].shape[0] // 4
    count = len(parts)

    def kernel(place_ref, *refs):
        own = place_ref[which]
        for hop in range(4):
            at = pl.ds(pl.multiple_of(((own + hop) & 3) * rows, rows), rows)
            total = refs[0][at, :]
            for ref in refs[1:count]:
                total = total + ref[at, :]
            refs[count + hop][...] = total

    return pl.pallas_call(
        kernel,
        in_specs=[pl.BlockSpec(memory_space=pltpu.SMEM)] + vmem_specs(count),
        out_specs=vmem_specs(4),
        out_shape=[jax.ShapeDtypeStruct((rows, 128), F32)] * 4,
        compiler_params=grant(4),
        name="sum_and_cut",
    )(place, *parts)


def sum_and_copy(parts, copies):
    count = len(parts)

    def kernel(*refs):
        total = refs[0][...]
        for ref in refs[1:count]:
            total = total + ref[...]
        for k in range(copies):
            refs[count][k] = total

    return pl.pallas_call(
        kernel,
        in_specs=vmem_specs(count),
        out_specs=vmem_specs(1)[0],
        out_shape=jax.ShapeDtypeStruct((copies,) + parts[0].shape, F32),
        compiler_params=grant(2),
    )(*parts)


def sum_scaled(parts, scale):
    def kernel(parts_ref, out_ref):
        total = parts_ref[0]
        for k in range(1, parts.shape[0]):
            total = total + parts_ref[k]
        out_ref[...] = total * scale

    return pl.pallas_call(
        kernel,
        in_specs=vmem_specs(1),
        out_specs=vmem_specs(1)[0],
        out_shape=jax.ShapeDtypeStruct(parts.shape[1:], F32),
        compiler_params=grant(2),
        name="sum_scaled",
    )(parts)


def assemble(place, which, parts):
    rows = parts[0].shape[0]

    def kernel(place_ref, *refs):
        own = place_ref[which]
        for hop in range(4):
            at = pl.ds(pl.multiple_of(((own - hop) & 3) * rows, rows), rows)
            refs[4][at, :] = refs[hop][...]

    return pl.pallas_call(
        kernel,
        in_specs=[pl.BlockSpec(memory_space=pltpu.SMEM)] + vmem_specs(4),
        out_specs=vmem_specs(1)[0],
        out_shape=jax.ShapeDtypeStruct((4 * rows, 128), F32),
        compiler_params=grant(2),
        name="assemble",
    )(place, *parts)


def final_weights(place, mine, theirs):
    rows = mine[0].shape[0]

    def kernel(place_ref, *refs):
        first_core, own = place_ref[1] == 0, place_ref[2]
        for hop in range(4):
            at = pl.ds(pl.multiple_of(((own - hop) & 3) * rows, rows), rows)
            here, there = refs[hop][...], refs[4 + hop][...]
            refs[8][at, 0:128] = jnp.where(first_core, here, there)
            refs[8][at, 128:256] = jnp.where(first_core, there, here)

    return pl.pallas_call(
        kernel,
        in_specs=[pl.BlockSpec(memory_space=pltpu.SMEM)] + vmem_specs(8),
        out_specs=vmem_specs(1)[0],
        out_shape=jax.ShapeDtypeStruct((4 * rows, 256), F32),
        compiler_params=grant(6),
        name="final_weights",
    )(place, *mine, *theirs)


def tile_kernel(
    live_ref, act_ref, cot_ref, weight_ref, halo_ref, feat_ref, grad_ref,
    even, odd, wide, tall, left, line, shift, around, mix, lines,
):
    live = live_ref[0].astype(F32)
    tall[...] = halo_ref[...].astype(F32).reshape(512, 128)
    first = tall[pl.ds(0, 32, stride=8), :]
    second = tall[pl.ds(1, 32, stride=8), :]
    line[8:40, :] = second
    line[7:8, :] = tall[4:5, :]
    even[0:32, 0:128] = line[7:39, :].astype(BF)
    even[0:32, 128:256] = first.astype(BF)
    even[0:32, 256:384] = second.astype(BF)
    left[0] = tall[pl.ds(256, 32, stride=8), :]
    left[1] = tall[pl.ds(257, 32, stride=8), :]
    fill_patches(act_ref, even, odd, wide, left)
    result = jnp.dot(even[0:1024, :], weight_ref[0:384, :], preferred_element_type=F32)
    result += jnp.dot(odd[...], weight_ref[384:768, :], preferred_element_type=F32)
    result += jnp.dot(even[32:1056, :], weight_ref[768:1152, :], preferred_element_type=F32)
    feat_ref[...] = (result * live).astype(BF).reshape(32, 32, 256)

    right = jnp.concatenate(
        [tall[pl.ds(258, 32, stride=8), :], tall[pl.ds(259, 32, stride=8), :]], axis=1
    )
    around[0:32, :] = right
    around[32:33, 0:128] = tall[5:6, :]
    around[32:33, 128:256] = tall[6:7, :]
    below = jnp.concatenate(
        [tall[pl.ds(2, 32, stride=8), :], tall[pl.ds(3, 32, stride=8), :]], axis=1
    )

    def place(i, values):
        shift[0:32, :] = values
        shift[32:33, :] = around[pl.ds(i, 1), :]
        at = pl.ds(pl.multiple_of(i * 32, 32), 32)
        mix[at, 0:256] = values.astype(BF)
        mix[at, 256:512] = shift[1:33, :].astype(BF)

    def one_row(i, carry):
        place(i, cot_ref[i].astype(F32))
        return carry

    lax.fori_loop(0, 32, one_row, 0, unroll=4)
    place(32, below)

    def tap(a, b):
        at = (3 * a + b) * 128
        return weight_ref[at : at + 128, :]

    none = jnp.zeros((128, 256), BF)

    def block(even_taps, odd_taps):
        return jnp.concatenate(
            [jnp.concatenate(even_taps, axis=1), jnp.concatenate(odd_taps, axis=1)], axis=0
        )

    def back(rows, matrix):
        return lax.dot_general(
            rows, matrix, (((1,), (1,)), ((), ())), preferred_element_type=F32
        )

    here, after = mix[0:1024, :], mix[32:1056, :]
    lines[0] = back(here, block([tap(1, 1), none], [tap(1, 2), tap(1, 0)])) * live
    lines[1] = (
        back(here, block([tap(2, 1), none], [tap(2, 2), tap(2, 0)]))
        + back(after, block([tap(0, 1), none], [tap(0, 2), tap(0, 0)]))
    ) * live

    def weave(i, carry):
        at = pl.ds(pl.multiple_of(i * 32, 32), 32)
        for parity in range(2):
            for side in range(2):
                wide[parity, pl.ds(8 + side, 32, stride=2), :] = lines[
                    parity, at, side * 128 : (side + 1) * 128
                ]
            grad_ref[2 * i + parity] = wide[parity, 8:72, :].astype(BF)
        return carry

    lax.fori_loop(0, 32, weave, 0, unroll=4)


def tile_terms(live, act, cot, weight_matrix, halo):
    return pl.pallas_call(
        tile_kernel,
        in_specs=[pl.BlockSpec(memory_space=pltpu.SMEM)] + vmem_specs(4),
        out_specs=vmem_specs(2),
        out_shape=[
            jax.ShapeDtypeStruct((32, 32, 256), BF),
            jax.ShapeDtypeStruct((64, 64, 128), BF),
        ],
        scratch_shapes=[
            pltpu.VMEM((1056, 384), BF),
            pltpu.VMEM((1024, 384), BF),
            pltpu.VMEM((2, 72, 128), F32),
            pltpu.VMEM((512, 128), F32),
            pltpu.VMEM((2, 32, 128), F32),
            pltpu.VMEM((40, 128), F32),
            pltpu.VMEM((40, 256), F32),
            pltpu.VMEM((40, 256), F32),
            pltpu.VMEM((1056, 512), BF),
            pltpu.VMEM((2, 1024, 256), F32),
        ],
        cost_estimate=pl.CostEstimate(
            flops=5 * 1024 * 1152 * 256, bytes_accessed=4 << 20, transcendentals=0
        ),
        compiler_params=grant(24),
        name="tile_terms",
    )(live, act, cot, weight_matrix, halo)


def shards(activations, cotangent, weights, tile_list):
    act, cot = activations[0, 0], cotangent[0, 0]
    slots = lax.axis_size("tiles")
    slides = lax.axis_size("slide")
    half_side = cot.shape[0]
    listing = tile_list[0]
    me = lax.axis_index("tiles")
    live = (lax.dynamic_slice_in_dim(listing, me, 1) >= 0).astype(jnp.int32)
    own = lax.axis_index("slide")
    step = jnp.where(me < slots // 2, 1, 3)
    place = jnp.stack([step, me & 1, own, (me >> 1) & 3]).astype(jnp.int32)
    select = halo_matrices(listing, me, slots // GW)
    weight_matrix = weights.reshape(-1, weights.shape[3])

    partner = [(t, t ^ 1) for t in range(slots)]
    columns = [[z * 8 + rest for z in range(8)] for rest in range(8)]

    def over_slide(values, hop):
        return lax.ppermute(values, "slide", [(i, (i + hop) % slides) for i in range(slides)])

    def over_x(values, hop):
        pairs = [(t, (t & ~6) | ((((t >> 1) + hop) & 3) << 1)) for t in range(slots)]
        return lax.ppermute(values, "tiles", pairs)

    pieces = lax.all_to_all(pack_edges(act, cot), "tiles", 0, 0, tiled=True)
    inner = interior_weights(live, act, cot)
    back, keep, send = turn_edges(place, pieces, select, inner)

    got = lax.ppermute(send, "tiles", partner)
    quarters = sum_and_cut(place, 2, [keep, got])
    moved = []
    for hop in range(1, 4):
        moved.append(over_slide(quarters[hop], hop))
    halo = lax.all_to_all(back, "tiles", 0, 0, tiled=True)
    cuts = sum_and_cut(place, 3, [quarters[0]] + moved)
    moved = []
    for hop in range(1, 4):
        moved.append(over_x(cuts[hop], hop))
    copies = sum_and_copy([cuts[0]] + moved, 8)
    copies, halo = lax.optimization_barrier((copies, halo))
    parts = lax.all_to_all(copies, "tiles", 0, 0, tiled=True, axis_index_groups=columns)
    grad_scale = 1.0 / math.sqrt(slides * slots * half_side * half_side)
    eighth = sum_scaled(parts, grad_scale)

    features_out, input_grad = tile_terms(live, act, cot, weight_matrix, halo)

    quarter = assemble(place, 3, [eighth] + [over_x(eighth, hop) for hop in range(1, 4)])
    mine = [quarter]
    for hop in range(1, 4):
        mine.append(over_slide(quarter, hop))
    theirs = []
    for hop in range(4):
        theirs.append(lax.ppermute(mine[hop], "tiles", partner))
    weight_grad = final_weights(place, mine, theirs).reshape(weights.shape)
    return (features_out[None, None], input_grad[None, None], weight_grad)


def solution(mesh):
    placed = (
        P("slide", "tiles", None, None, None),
        P("slide", "tiles", None, None, None),
        P(),
        P("slide", None),
    )
    return jax.shard_map(
        shards,
        mesh=mesh,
        in_specs=placed,
        out_specs=(
            P("slide", "tiles", None, None, None),
            P("slide", "tiles", None, None, None),
            P(),
        ),
        check_vma=False,
    )
```

```python
import math

import jax
import jax.numpy as jnp
from jax import lax
from jax.experimental import pallas as pl
from jax.experimental.pallas import tpu as pltpu
from jax.sharding import PartitionSpec as P


GW = 8
BF = jnp.bfloat16
F32 = jnp.float32


def grant(mebibytes):
    return pltpu.CompilerParams(vmem_limit_bytes=mebibytes << 20)


def vmem_specs(count):
    return [pl.BlockSpec(memory_space=pltpu.VMEM)] * count


def halo_matrices(listing, me, grid_rows):
    row, col = listing // GW, listing % GW
    live = listing >= 0

    def chosen(row_step, col_step):
        new_row, new_col = row + row_step, col + col_step
        inside = live & (new_row >= 0) & (new_row < grid_rows) & (new_col >= 0) & (new_col < GW)
        target = jnp.where(inside, new_row * GW + new_col, -2)
        return listing[None, :] == target[:, None]

    half = listing.shape[0] // 2
    by_row = me < half
    act = jnp.where(by_row, chosen(-1, 0), chosen(0, -1))
    cot = jnp.where(by_row, chosen(1, 0), chosen(0, 1))
    diag = chosen(-1, -1)
    below_right = chosen(1, 1)
    before = jnp.where(me == 0, diag, act & (me != half))
    return jnp.stack([before, act, cot, diag, below_right]).astype(BF)


def pack_kernel(
    act_ref, cot_ref, out_ref, row_buf, col_buf, crow_buf, ccol_buf, sems, tall, line, both
):
    copies = [
        pltpu.make_async_copy(act_ref.at[63], row_buf, sems.at[0]),
        pltpu.make_async_copy(act_ref.at[:, 56:64, :], col_buf, sems.at[1]),
        pltpu.make_async_copy(cot_ref.at[0], crow_buf, sems.at[2]),
        pltpu.make_async_copy(cot_ref.at[:, 0:8, :], ccol_buf, sems.at[3]),
    ]
    for copy in copies:
        copy.start()

    def fill(base, values, cot_values):
        line[8:72, :] = values
        line[7:8, :] = values[63:64, :]
        for slot in range(3):
            both[pl.ds(base * 8 + slot, 32, stride=8), :] = line[pl.ds(7 + slot, 32, stride=2), :]
        both[pl.ds(base * 8 + 3, 32, stride=8), :] = cot_values[:, 0:128]
        both[pl.ds(base * 8 + 4, 32, stride=8), :] = cot_values[:, 128:256]

    both[...] = jnp.zeros_like(both)
    for copy in copies:
        copy.wait()
    fill(0, row_buf[...].astype(F32), crow_buf[...].astype(F32))
    tall[...] = col_buf[...].astype(F32).reshape(512, 128)
    values = tall[pl.ds(7, 64, stride=8), :]
    tall[0:256, :] = ccol_buf[:, :, 0:128].astype(F32).reshape(256, 128)
    tall[256:512, :] = ccol_buf[:, :, 128:256].astype(F32).reshape(256, 128)
    low = tall[pl.ds(0, 32, stride=8), :]
    high = tall[pl.ds(256, 32, stride=8), :]
    fill(32, values, jnp.concatenate([low, high], axis=1))
    out_ref[...] = both[...].reshape(64, 8, 128).astype(BF)


def pack_edges(act, cot):
    return pl.pallas_call(
        pack_kernel,
        in_specs=[pl.BlockSpec(memory_space=pltpu.HBM)] * 2,
        out_specs=vmem_specs(1)[0],
        out_shape=jax.ShapeDtypeStruct((64, 8, 128), BF),
        scratch_shapes=[
            pltpu.VMEM((64, 128), BF),
            pltpu.VMEM((64, 8, 128), BF),
            pltpu.VMEM((32, 256), BF),
            pltpu.VMEM((32, 8, 256), BF),
            pltpu.SemaphoreType.DMA((4,)),
            pltpu.VMEM((512, 128), F32),
            pltpu.VMEM((72, 128), F32),
            pltpu.VMEM((512, 128), F32),
        ],
        name="pack_edges",
    )(act, cot)


def fill_patches(act_ref, even, odd, wide, left):
    def one_row(i, carry):
        for parity in range(2):
            p = 2 * i + parity
            wide[parity, 8:72, :] = act_ref[p].astype(F32)
            if left is not None:
                wide[parity, 7:8, :] = left[parity, pl.ds(i, 1), :]
        for parity in range(2):
            dest = odd if parity == 0 else even
            start = pl.multiple_of((i + parity) * 32, 32)
            for b in range(3):
                dest[pl.ds(start, 32), b * 128 : (b + 1) * 128] = wide[
                    parity, pl.ds(7 + b, 32, stride=2), :
                ].astype(BF)
        return carry

    lax.fori_loop(0, 32, one_row, 0, unroll=4)


def weight_kernel(place_ref, act_ref, cot_ref, keep_ref, send_ref, even, odd, wide):
    even[0:32, :] = jnp.zeros((32, 384), BF)
    for parity in range(2):
        wide[parity, 0:8, :] = jnp.zeros((8, 128), F32)
    fill_patches(act_ref, even, odd, wide, None)
    live = place_ref[4].astype(F32).astype(BF)
    first_core = place_ref[1] == 0
    cot = cot_ref[...].reshape(1024, 256) * live
    for a, rows in enumerate((even[0:1024, :], odd[...], even[32:1056, :])):
        terms = lax.dot_general(
            rows, cot, (((0,), (0,)), ((), ())), preferred_element_type=F32
        )
        at = slice(a * 384, (a + 1) * 384)
        keep_ref[at, :] = jnp.where(first_core, terms[:, 0:128], terms[:, 128:256])
        send_ref[at, :] = jnp.where(first_core, terms[:, 128:256], terms[:, 0:128])


def interior_weights(place, act, cot):
    return pl.pallas_call(
        weight_kernel,
        in_specs=[pl.BlockSpec(memory_space=pltpu.SMEM)] + vmem_specs(2),
        out_specs=vmem_specs(2),
        out_shape=[jax.ShapeDtypeStruct((1152, 128), F32)] * 2,
        scratch_shapes=[
            pltpu.VMEM((1056, 384), BF),
            pltpu.VMEM((1024, 384), BF),
            pltpu.VMEM((2, 72, 128), F32),
        ],
        cost_estimate=pl.CostEstimate(
            flops=2 * 1024 * 1152 * 256, bytes_accessed=3 << 20, transcendentals=0
        ),
        compiler_params=grant(12),
        name="interior_weights",
    )(place, act, cot)


def turn_kernel(
    place_ref, pieces_ref, select_ref, back_ref, keep_ref, send_ref, tall
):
    tall[...] = pieces_ref[...].astype(F32).reshape(512, 128)
    slots = [tall[pl.ds(slot, 64, stride=8), :].astype(BF) for slot in range(5)]
    cot = jnp.concatenate(slots[3:5], axis=1)

    def pick(which, values):
        return jnp.dot(select_ref[which], values, preferred_element_type=F32)

    before, first, second = pick(0, slots[0]), pick(1, slots[1]), pick(1, slots[2])
    returned = pick(2, cot)
    corner = pick(4, cot)
    tall[pl.ds(0, 64, stride=8), :] = first
    tall[pl.ds(1, 64, stride=8), :] = second
    tall[pl.ds(2, 64, stride=8), :] = returned[:, 0:128]
    tall[pl.ds(3, 64, stride=8), :] = returned[:, 128:256]
    tall[pl.ds(4, 64, stride=8), :] = pick(3, slots[0])
    tall[pl.ds(5, 64, stride=8), :] = corner[:, 0:128]
    tall[pl.ds(6, 64, stride=8), :] = corner[:, 128:256]
    tall[pl.ds(7, 64, stride=8), :] = corner[:, 0:128]
    back_ref[...] = tall[...].reshape(64, 8, 128).astype(BF)
    first_core = place_ref[1] == 0
    for b, values in enumerate((before, first, second)):
        terms = lax.dot_general(
            values.astype(BF), cot, (((0,), (0,)), ((), ())), preferred_element_type=F32
        )
        keep_ref[b] = jnp.where(first_core, terms[:, 0:128], terms[:, 128:256])
        send_ref[b] = jnp.where(first_core, terms[:, 128:256], terms[:, 0:128])


def turn_edges(place, pieces, select):
    return pl.pallas_call(
        turn_kernel,
        in_specs=[pl.BlockSpec(memory_space=pltpu.SMEM)] + vmem_specs(2),
        out_specs=vmem_specs(3),
        out_shape=[
            jax.ShapeDtypeStruct((64, 8, 128), BF),
            jax.ShapeDtypeStruct((3, 128, 128), F32),
            jax.ShapeDtypeStruct((3, 128, 128), F32),
        ],
        scratch_shapes=[pltpu.VMEM((512, 128), F32)],
        compiler_params=grant(10),
        name="turn_edges",
    )(place, pieces, select)


def join_and_cut(place, keep, got, edges, got_edges):
    rows = keep.shape[0] // 4

    def kernel(place_ref, keep_ref, got_ref, edge_ref, got_edge_ref, *refs):
        total = refs[4]
        total[...] = keep_ref[...] + got_ref[...]
        for b in range(3):
            at = pl.ds(pl.multiple_of(b * place_ref[0] * 128, 128), 128)
            total[at, :] = total[at, :] + (edge_ref[b] + got_edge_ref[b])
        own = place_ref[2]
        for hop in range(4):
            at = pl.ds(pl.multiple_of(((own + hop) & 3) * rows, rows), rows)
            refs[hop][...] = total[at, :]

    return pl.pallas_call(
        kernel,
        in_specs=[pl.BlockSpec(memory_space=pltpu.SMEM)] + vmem_specs(4),
        out_specs=vmem_specs(4),
        out_shape=[jax.ShapeDtypeStruct((rows, 128), F32)] * 4,
        scratch_shapes=[pltpu.VMEM((4 * rows, 128), F32)],
        compiler_params=grant(6),
        name="join_and_cut",
    )(place, keep, got, edges, got_edges)


def sum_and_cut(place, which, parts):
    rows = parts[0].shape[0] // 4
    count = len(parts)

    def kernel(place_ref, *refs):
        own = place_ref[which]
        for hop in range(4):
            at = pl.ds(pl.multiple_of(((own + hop) & 3) * rows, rows), rows)
            total = refs[0][at, :]
            for ref in refs[1:count]:
                total = total + ref[at, :]
            refs[count + hop][...] = total

    return pl.pallas_call(
        kernel,
        in_specs=[pl.BlockSpec(memory_space=pltpu.SMEM)] + vmem_specs(count),
        out_specs=vmem_specs(4),
        out_shape=[jax.ShapeDtypeStruct((rows, 128), F32)] * 4,
        compiler_params=grant(4),
        name="sum_and_cut",
    )(place, *parts)


def sum_and_copy(parts, copies):
    count = len(parts)

    def kernel(*refs):
        total = refs[0][...]
        for ref in refs[1:count]:
            total = total + ref[...]
        for k in range(copies):
            refs[count][k] = total

    return pl.pallas_call(
        kernel,
        in_specs=vmem_specs(count),
        out_specs=vmem_specs(1)[0],
        out_shape=jax.ShapeDtypeStruct((copies,) + parts[0].shape, F32),
        compiler_params=grant(2),
    )(*parts)


def sum_scaled(parts, scale):
    def kernel(parts_ref, out_ref):
        total = parts_ref[0]
        for k in range(1, parts.shape[0]):
            total = total + parts_ref[k]
        out_ref[...] = total * scale

    return pl.pallas_call(
        kernel,
        in_specs=vmem_specs(1),
        out_specs=vmem_specs(1)[0],
        out_shape=jax.ShapeDtypeStruct(parts.shape[1:], F32),
        compiler_params=grant(2),
        name="sum_scaled",
    )(parts)


def assemble(place, which, parts):
    rows = parts[0].shape[0]

    def kernel(place_ref, *refs):
        own = place_ref[which]
        for hop in range(4):
            at = pl.ds(pl.multiple_of(((own - hop) & 3) * rows, rows), rows)
            refs[4][at, :] = refs[hop][...]

    return pl.pallas_call(
        kernel,
        in_specs=[pl.BlockSpec(memory_space=pltpu.SMEM)] + vmem_specs(4),
        out_specs=vmem_specs(1)[0],
        out_shape=jax.ShapeDtypeStruct((4 * rows, 128), F32),
        compiler_params=grant(2),
        name="assemble",
    )(place, *parts)


def final_weights(place, mine, theirs):
    rows = mine[0].shape[0]

    def kernel(place_ref, *refs):
        core, own = place_ref[1], place_ref[2]
        out_ref, sems = refs[8], refs[9]
        copies = []
        for side in range(2):
            half = core if side == 0 else 1 - core
            columns = pl.ds(pl.multiple_of(half * 128, 128), 128)
            for hop in range(4):
                at = pl.ds(pl.multiple_of(((own - hop) & 3) * rows, rows), rows)
                k = 4 * side + hop
                copies.append(
                    pltpu.make_async_copy(refs[k], out_ref.at[at, columns], sems.at[k])
                )
                copies[-1].start()
        for copy in copies:
            copy.wait()

    return pl.pallas_call(
        kernel,
        in_specs=[pl.BlockSpec(memory_space=pltpu.SMEM)] + vmem_specs(8),
        out_specs=pl.BlockSpec(memory_space=pl.ANY),
        out_shape=jax.ShapeDtypeStruct((4 * rows, 256), F32),
        scratch_shapes=[pltpu.SemaphoreType.DMA((8,))],
        compiler_params=grant(6),
        name="final_weights",
    )(place, *mine, *theirs)


def feature_kernel(
    live_ref, act_ref, weight_ref, halo_ref, feat_ref, even, odd, wide, tall, left, line
):
    live = live_ref[0].astype(F32)
    tall[...] = halo_ref[...].astype(F32).reshape(512, 128)
    first = tall[pl.ds(0, 32, stride=8), :]
    second = tall[pl.ds(1, 32, stride=8), :]
    line[8:40, :] = second
    line[7:8, :] = tall[4:5, :]
    even[0:32, 0:128] = line[7:39, :].astype(BF)
    even[0:32, 128:256] = first.astype(BF)
    even[0:32, 256:384] = second.astype(BF)
    left[0] = tall[pl.ds(256, 32, stride=8), :]
    left[1] = tall[pl.ds(257, 32, stride=8), :]
    fill_patches(act_ref, even, odd, wide, left)
    result = jnp.dot(even[0:1024, :], weight_ref[0:384, :], preferred_element_type=F32)
    result += jnp.dot(odd[...], weight_ref[384:768, :], preferred_element_type=F32)
    result += jnp.dot(even[32:1056, :], weight_ref[768:1152, :], preferred_element_type=F32)
    feat_ref[...] = (result * live).astype(BF).reshape(32, 32, 256)


def tile_features(live, act, weight_matrix, halo):
    return pl.pallas_call(
        feature_kernel,
        in_specs=[pl.BlockSpec(memory_space=pltpu.SMEM)] + vmem_specs(3),
        out_specs=vmem_specs(1)[0],
        out_shape=jax.ShapeDtypeStruct((32, 32, 256), BF),
        scratch_shapes=[
            pltpu.VMEM((1056, 384), BF),
            pltpu.VMEM((1024, 384), BF),
            pltpu.VMEM((2, 72, 128), F32),
            pltpu.VMEM((512, 128), F32),
            pltpu.VMEM((2, 32, 128), F32),
            pltpu.VMEM((40, 128), F32),
        ],
        cost_estimate=pl.CostEstimate(
            flops=2 * 1024 * 1152 * 256, bytes_accessed=2 << 20, transcendentals=0
        ),
        compiler_params=grant(16),
        name="tile_features",
    )(live, act, weight_matrix, halo)


def gradient_kernel(
    live_ref, cot_ref, weight_ref, halo_ref, grad_ref, wide, tall, shift, around, mix, lines
):
    live = live_ref[0].astype(F32)
    tall[...] = halo_ref[...].astype(F32).reshape(512, 128)

    right = jnp.concatenate(
        [tall[pl.ds(258, 32, stride=8), :], tall[pl.ds(259, 32, stride=8), :]], axis=1
    )
    around[0:32, :] = right
    around[32:33, 0:128] = tall[5:6, :]
    around[32:33, 128:256] = tall[6:7, :]
    below = jnp.concatenate(
        [tall[pl.ds(2, 32, stride=8), :], tall[pl.ds(3, 32, stride=8), :]], axis=1
    )

    def place(i, values):
        shift[0:32, :] = values
        shift[32:33, :] = around[pl.ds(i, 1), :]
        at = pl.ds(pl.multiple_of(i * 32, 32), 32)
        mix[at, 0:256] = values.astype(BF)
        mix[at, 256:512] = shift[1:33, :].astype(BF)

    def one_row(i, carry):
        place(i, cot_ref[i].astype(F32))
        return carry

    lax.fori_loop(0, 32, one_row, 0, unroll=4)
    place(32, below)

    def tap(a, b):
        at = (3 * a + b) * 128
        return weight_ref[at : at + 128, :]

    none = jnp.zeros((128, 256), BF)

    def block(even_taps, odd_taps):
        return jnp.concatenate(
            [jnp.concatenate(even_taps, axis=1), jnp.concatenate(odd_taps, axis=1)], axis=0
        )

    def back(rows, matrix):
        return lax.dot_general(
            rows, matrix, (((1,), (1,)), ((), ())), preferred_element_type=F32
        )

    here, after = mix[0:1024, :], mix[32:1056, :]
    lines[0] = back(here, block([tap(1, 1), none], [tap(1, 2), tap(1, 0)])) * live
    lines[1] = (
        back(here, block([tap(2, 1), none], [tap(2, 2), tap(2, 0)]))
        + back(after, block([tap(0, 1), none], [tap(0, 2), tap(0, 0)]))
    ) * live

    def weave(i, carry):
        at = pl.ds(pl.multiple_of(i * 32, 32), 32)
        for parity in range(2):
            for side in range(2):
                wide[parity, pl.ds(8 + side, 32, stride=2), :] = lines[
                    parity, at, side * 128 : (side + 1) * 128
                ]
            grad_ref[2 * i + parity] = wide[parity, 8:72, :].astype(BF)
        return carry

    lax.fori_loop(0, 32, weave, 0, unroll=4)


def tile_gradient(live, cot, weight_matrix, halo):
    return pl.pallas_call(
        gradient_kernel,
        in_specs=[pl.BlockSpec(memory_space=pltpu.SMEM)] + vmem_specs(3),
        out_specs=vmem_specs(1)[0],
        out_shape=jax.ShapeDtypeStruct((64, 64, 128), BF),
        scratch_shapes=[
            pltpu.VMEM((2, 72, 128), F32),
            pltpu.VMEM((512, 128), F32),
            pltpu.VMEM((40, 256), F32),
            pltpu.VMEM((40, 256), F32),
            pltpu.VMEM((1056, 512), BF),
            pltpu.VMEM((2, 1024, 256), F32),
        ],
        cost_estimate=pl.CostEstimate(
            flops=3 * 1024 * 1152 * 256, bytes_accessed=3 << 20, transcendentals=0
        ),
        compiler_params=grant(20),
        name="tile_gradient",
    )(live, cot, weight_matrix, halo)


def shards(activations, cotangent, weights, tile_list):
    act, cot = activations[0, 0], cotangent[0, 0]
    slots = lax.axis_size("tiles")
    slides = lax.axis_size("slide")
    half_side = cot.shape[0]
    listing = tile_list[0]
    me = lax.axis_index("tiles")
    live = (lax.dynamic_slice_in_dim(listing, me, 1) >= 0).astype(jnp.int32)
    own = lax.axis_index("slide")
    step = jnp.where(me < slots // 2, 1, 3)
    place = jnp.stack([step, me & 1, own, (me >> 1) & 3, live[0]]).astype(jnp.int32)
    select = halo_matrices(listing, me, slots // GW)
    weight_matrix = weights.reshape(-1, weights.shape[3])

    partner = [(t, t ^ 1) for t in range(slots)]
    columns = [[z * 8 + rest for z in range(8)] for rest in range(8)]

    def over_slide(values, hop):
        return lax.ppermute(values, "slide", [(i, (i + hop) % slides) for i in range(slides)])

    def over_x(values, hop):
        pairs = [(t, (t & ~6) | ((((t >> 1) + hop) & 3) << 1)) for t in range(slots)]
        return lax.ppermute(values, "tiles", pairs)

    pieces = lax.all_to_all(pack_edges(act, cot), "tiles", 0, 0, tiled=True)
    keep, send = interior_weights(place, act, cot)
    got = lax.ppermute(send, "tiles", partner)
    back, edges, send_edges = turn_edges(place, pieces, select)

    got_edges = lax.ppermute(send_edges, "tiles", partner)
    quarters = join_and_cut(place, keep, got, edges, got_edges)
    moved = []
    for hop in range(1, 4):
        moved.append(over_slide(quarters[hop], hop))
    halo = lax.all_to_all(back, "tiles", 0, 0, tiled=True)
    cuts = sum_and_cut(place, 3, [quarters[0]] + moved)
    moved = []
    for hop in range(1, 4):
        moved.append(over_x(cuts[hop], hop))
    copies = sum_and_copy([cuts[0]] + moved, 8)
    copies, halo = lax.optimization_barrier((copies, halo))
    parts = lax.all_to_all(copies, "tiles", 0, 0, tiled=True, axis_index_groups=columns)
    grad_scale = 1.0 / math.sqrt(slides * slots * half_side * half_side)
    eighth = sum_scaled(parts, grad_scale)

    features_out = tile_features(live, act, weight_matrix, halo)
    input_grad = tile_gradient(live, cot, weight_matrix, halo)

    eighths = [eighth]
    for hop in range(1, 4):
        eighths.append(over_x(eighth, hop))
    quarter = assemble(place, 3, eighths)
    mine = [quarter]
    for hop in range(1, 4):
        mine.append(over_slide(quarter, hop))
    theirs = []
    for hop in range(4):
        theirs.append(lax.ppermute(mine[hop], "tiles", partner))
    weight_grad = final_weights(place, mine, theirs).reshape(weights.shape)
    return (features_out[None, None], input_grad[None, None], weight_grad)


def solution(mesh):
    placed = (
        P("slide", "tiles", None, None, None),
        P("slide", "tiles", None, None, None),
        P(),
        P("slide", None),
    )
    return jax.shard_map(
        shards,
        mesh=mesh,
        in_specs=placed,
        out_specs=(
            P("slide", "tiles", None, None, None),
            P("slide", "tiles", None, None, None),
            P(),
        ),
        check_vma=False,
    )
```

```python
import math

import jax
import jax.numpy as jnp
from jax import lax
from jax.experimental import pallas as pl
from jax.experimental.pallas import tpu as pltpu
from jax.sharding import PartitionSpec as P


GW = 8
BF = jnp.bfloat16
F32 = jnp.float32


def grant(mebibytes):
    return pltpu.CompilerParams(vmem_limit_bytes=mebibytes << 20)


def vmem_specs(count):
    return [pl.BlockSpec(memory_space=pltpu.VMEM)] * count


def halo_matrices(listing, me, grid_rows):
    row, col = listing // GW, listing % GW
    live = listing >= 0

    def chosen(row_step, col_step):
        new_row, new_col = row + row_step, col + col_step
        inside = live & (new_row >= 0) & (new_row < grid_rows) & (new_col >= 0) & (new_col < GW)
        target = jnp.where(inside, new_row * GW + new_col, -2)
        return listing[None, :] == target[:, None]

    half = listing.shape[0] // 2
    by_row = me < half
    act = jnp.where(by_row, chosen(-1, 0), chosen(0, -1))
    cot = jnp.where(by_row, chosen(1, 0), chosen(0, 1))
    diag = chosen(-1, -1)
    below_right = chosen(1, 1)
    before = jnp.where(me == 0, diag, act & (me != half))
    return jnp.stack([before, act, cot, diag, below_right]).astype(BF)


def pack_kernel(
    act_ref, cot_ref, out_ref, row_buf, col_buf, crow_buf, ccol_buf, sems, tall, line, both
):
    copies = [
        pltpu.make_async_copy(act_ref.at[63], row_buf, sems.at[0]),
        pltpu.make_async_copy(act_ref.at[:, 56:64, :], col_buf, sems.at[1]),
        pltpu.make_async_copy(cot_ref.at[0], crow_buf, sems.at[2]),
        pltpu.make_async_copy(cot_ref.at[:, 0:8, :], ccol_buf, sems.at[3]),
    ]
    for copy in copies:
        copy.start()

    def fill(base, values, cot_values):
        line[8:72, :] = values
        line[7:8, :] = values[63:64, :]
        for slot in range(3):
            both[pl.ds(base * 8 + slot, 32, stride=8), :] = line[pl.ds(7 + slot, 32, stride=2), :]
        both[pl.ds(base * 8 + 3, 32, stride=8), :] = cot_values[:, 0:128]
        both[pl.ds(base * 8 + 4, 32, stride=8), :] = cot_values[:, 128:256]

    both[...] = jnp.zeros_like(both)
    for copy in copies:
        copy.wait()
    fill(0, row_buf[...].astype(F32), crow_buf[...].astype(F32))
    tall[...] = col_buf[...].astype(F32).reshape(512, 128)
    values = tall[pl.ds(7, 64, stride=8), :]
    tall[0:256, :] = ccol_buf[:, :, 0:128].astype(F32).reshape(256, 128)
    tall[256:512, :] = ccol_buf[:, :, 128:256].astype(F32).reshape(256, 128)
    low = tall[pl.ds(0, 32, stride=8), :]
    high = tall[pl.ds(256, 32, stride=8), :]
    fill(32, values, jnp.concatenate([low, high], axis=1))
    out_ref[...] = both[...].reshape(64, 8, 128).astype(BF)


def pack_edges(act, cot):
    return pl.pallas_call(
        pack_kernel,
        in_specs=[pl.BlockSpec(memory_space=pltpu.HBM)] * 2,
        out_specs=vmem_specs(1)[0],
        out_shape=jax.ShapeDtypeStruct((64, 8, 128), BF),
        scratch_shapes=[
            pltpu.VMEM((64, 128), BF),
            pltpu.VMEM((64, 8, 128), BF),
            pltpu.VMEM((32, 256), BF),
            pltpu.VMEM((32, 8, 256), BF),
            pltpu.SemaphoreType.DMA((4,)),
            pltpu.VMEM((512, 128), F32),
            pltpu.VMEM((72, 128), F32),
            pltpu.VMEM((512, 128), F32),
        ],
        compiler_params=grant(60),
        name="pack_edges",
    )(act, cot)


def fill_patches(act_ref, even, odd, wide, left):
    def one_row(i, carry):
        for parity in range(2):
            p = 2 * i + parity
            wide[parity, 8:72, :] = act_ref[p].astype(F32)
            if left is not None:
                wide[parity, 7:8, :] = left[parity, pl.ds(i, 1), :]
        for parity in range(2):
            dest = odd if parity == 0 else even
            start = pl.multiple_of((i + parity) * 32, 32)
            for b in range(3):
                dest[pl.ds(start, 32), b * 128 : (b + 1) * 128] = wide[
                    parity, pl.ds(7 + b, 32, stride=2), :
                ].astype(BF)
        return carry

    lax.fori_loop(0, 32, one_row, 0, unroll=4)


def weight_kernel(place_ref, act_ref, cot_ref, keep_ref, send_ref, even, odd, wide):
    even[0:32, :] = jnp.zeros((32, 384), BF)
    for parity in range(2):
        wide[parity, 0:8, :] = jnp.zeros((8, 128), F32)
    fill_patches(act_ref, even, odd, wide, None)
    live = place_ref[4].astype(F32).astype(BF)
    first_core = place_ref[1] == 0
    cot = cot_ref[...].reshape(1024, 256) * live
    for a, rows in enumerate((even[0:1024, :], odd[...], even[32:1056, :])):
        terms = lax.dot_general(
            rows, cot, (((0,), (0,)), ((), ())), preferred_element_type=F32
        )
        at = slice(a * 384, (a + 1) * 384)
        keep_ref[at, :] = jnp.where(first_core, terms[:, 0:128], terms[:, 128:256])
        send_ref[at, :] = jnp.where(first_core, terms[:, 128:256], terms[:, 0:128])


def interior_weights(place, act, cot):
    return pl.pallas_call(
        weight_kernel,
        in_specs=[pl.BlockSpec(memory_space=pltpu.SMEM)] + vmem_specs(2),
        out_specs=vmem_specs(2),
        out_shape=[jax.ShapeDtypeStruct((1152, 128), F32)] * 2,
        scratch_shapes=[
            pltpu.VMEM((1056, 384), BF),
            pltpu.VMEM((1024, 384), BF),
            pltpu.VMEM((2, 72, 128), F32),
        ],
        cost_estimate=pl.CostEstimate(
            flops=2 * 1024 * 1152 * 256, bytes_accessed=3 << 20, transcendentals=0
        ),
        compiler_params=grant(12),
        name="interior_weights",
    )(place, act, cot)


def pick(select, values):
    return jnp.dot(select, values, preferred_element_type=F32)


def edge_kernel(place_ref, pieces_ref, select_ref, keep_ref, send_ref, tall):
    tall[...] = pieces_ref[...].astype(F32).reshape(512, 128)
    slots = [tall[pl.ds(slot, 64, stride=8), :].astype(BF) for slot in range(5)]
    cot = jnp.concatenate(slots[3:5], axis=1)
    first_core = place_ref[1] == 0
    for b in range(3):
        values = pick(select_ref[min(b, 1)], slots[b]).astype(BF)
        terms = lax.dot_general(
            values, cot, (((0,), (0,)), ((), ())), preferred_element_type=F32
        )
        keep_ref[b] = jnp.where(first_core, terms[:, 0:128], terms[:, 128:256])
        send_ref[b] = jnp.where(first_core, terms[:, 128:256], terms[:, 0:128])


def edge_weights(place, pieces, select):
    return pl.pallas_call(
        edge_kernel,
        in_specs=[pl.BlockSpec(memory_space=pltpu.SMEM)] + vmem_specs(2),
        out_specs=vmem_specs(2),
        out_shape=[jax.ShapeDtypeStruct((3, 128, 128), F32)] * 2,
        scratch_shapes=[pltpu.VMEM((512, 128), F32)],
        compiler_params=grant(6),
        name="edge_weights",
    )(place, pieces, select)


def turn_kernel(pieces_ref, select_ref, back_ref, tall):
    tall[...] = pieces_ref[...].astype(F32).reshape(512, 128)
    slots = [tall[pl.ds(slot, 64, stride=8), :].astype(BF) for slot in range(5)]
    cot = jnp.concatenate(slots[3:5], axis=1)
    returned = pick(select_ref[2], cot)
    corner = pick(select_ref[4], cot)
    tall[pl.ds(0, 64, stride=8), :] = pick(select_ref[1], slots[1])
    tall[pl.ds(1, 64, stride=8), :] = pick(select_ref[1], slots[2])
    tall[pl.ds(2, 64, stride=8), :] = returned[:, 0:128]
    tall[pl.ds(3, 64, stride=8), :] = returned[:, 128:256]
    tall[pl.ds(4, 64, stride=8), :] = pick(select_ref[3], slots[0])
    tall[pl.ds(5, 64, stride=8), :] = corner[:, 0:128]
    tall[pl.ds(6, 64, stride=8), :] = corner[:, 128:256]
    tall[pl.ds(7, 64, stride=8), :] = corner[:, 0:128]
    back_ref[...] = tall[...].reshape(64, 8, 128).astype(BF)


def turn_edges(pieces, select):
    return pl.pallas_call(
        turn_kernel,
        in_specs=vmem_specs(2),
        out_specs=vmem_specs(1)[0],
        out_shape=jax.ShapeDtypeStruct((64, 8, 128), BF),
        scratch_shapes=[pltpu.VMEM((512, 128), F32)],
        compiler_params=grant(6),
        name="turn_edges",
    )(pieces, select)


def join_and_cut(place, keep, got, edges, got_edges):
    rows = keep.shape[0] // 4

    def kernel(place_ref, keep_ref, got_ref, edge_ref, got_edge_ref, *refs):
        total = refs[4]
        total[...] = keep_ref[...] + got_ref[...]
        for b in range(3):
            at = pl.ds(pl.multiple_of(b * place_ref[0] * 128, 128), 128)
            total[at, :] = total[at, :] + (edge_ref[b] + got_edge_ref[b])
        own = place_ref[2]
        for hop in range(4):
            at = pl.ds(pl.multiple_of(((own + hop) & 3) * rows, rows), rows)
            refs[hop][...] = total[at, :]

    return pl.pallas_call(
        kernel,
        in_specs=[pl.BlockSpec(memory_space=pltpu.SMEM)] + vmem_specs(4),
        out_specs=vmem_specs(4),
        out_shape=[jax.ShapeDtypeStruct((rows, 128), F32)] * 4,
        scratch_shapes=[pltpu.VMEM((4 * rows, 128), F32)],
        compiler_params=grant(6),
        name="join_and_cut",
    )(place, keep, got, edges, got_edges)


def sum_and_cut(place, which, parts):
    rows = parts[0].shape[0] // 4
    count = len(parts)

    def kernel(place_ref, *refs):
        own = place_ref[which]
        for hop in range(4):
            at = pl.ds(pl.multiple_of(((own + hop) & 3) * rows, rows), rows)
            total = refs[0][at, :]
            for ref in refs[1:count]:
                total = total + ref[at, :]
            refs[count + hop][...] = total

    return pl.pallas_call(
        kernel,
        in_specs=[pl.BlockSpec(memory_space=pltpu.SMEM)] + vmem_specs(count),
        out_specs=vmem_specs(4),
        out_shape=[jax.ShapeDtypeStruct((rows, 128), F32)] * 4,
        compiler_params=grant(4),
        name="sum_and_cut",
    )(place, *parts)


def sum_and_copy(parts, copies):
    count = len(parts)

    def kernel(*refs):
        total = refs[0][...]
        for ref in refs[1:count]:
            total = total + ref[...]
        for k in range(copies):
            refs[count][k] = total

    return pl.pallas_call(
        kernel,
        in_specs=vmem_specs(count),
        out_specs=vmem_specs(1)[0],
        out_shape=jax.ShapeDtypeStruct((copies,) + parts[0].shape, F32),
        compiler_params=grant(2),
    )(*parts)


def sum_scaled(parts, scale):
    def kernel(parts_ref, out_ref):
        total = parts_ref[0]
        for k in range(1, parts.shape[0]):
            total = total + parts_ref[k]
        out_ref[...] = total * scale

    return pl.pallas_call(
        kernel,
        in_specs=vmem_specs(1),
        out_specs=vmem_specs(1)[0],
        out_shape=jax.ShapeDtypeStruct(parts.shape[1:], F32),
        compiler_params=grant(2),
        name="sum_scaled",
    )(parts)


def assemble(place, which, parts):
    rows = parts[0].shape[0]

    def kernel(place_ref, *refs):
        own = place_ref[which]
        for hop in range(4):
            at = pl.ds(pl.multiple_of(((own - hop) & 3) * rows, rows), rows)
            refs[4][at, :] = refs[hop][...]

    return pl.pallas_call(
        kernel,
        in_specs=[pl.BlockSpec(memory_space=pltpu.SMEM)] + vmem_specs(4),
        out_specs=vmem_specs(1)[0],
        out_shape=jax.ShapeDtypeStruct((4 * rows, 128), F32),
        compiler_params=grant(2),
        name="assemble",
    )(place, *parts)


def final_weights(place, mine, theirs):
    rows = mine[0].shape[0]

    def kernel(place_ref, *refs):
        core, own = place_ref[1], place_ref[2]
        out_ref, sems = refs[8], refs[9]
        copies = []
        for side in range(2):
            half = core if side == 0 else 1 - core
            columns = pl.ds(pl.multiple_of(half * 128, 128), 128)
            for hop in range(4):
                at = pl.ds(pl.multiple_of(((own - hop) & 3) * rows, rows), rows)
                k = 4 * side + hop
                copies.append(
                    pltpu.make_async_copy(refs[k], out_ref.at[at, columns], sems.at[k])
                )
                copies[-1].start()
        for copy in copies:
            copy.wait()

    return pl.pallas_call(
        kernel,
        in_specs=[pl.BlockSpec(memory_space=pltpu.SMEM)] + vmem_specs(8),
        out_specs=pl.BlockSpec(memory_space=pl.ANY),
        out_shape=jax.ShapeDtypeStruct((4 * rows, 256), F32),
        scratch_shapes=[pltpu.SemaphoreType.DMA((8,))],
        compiler_params=grant(6),
        name="final_weights",
    )(place, *mine, *theirs)


def feature_kernel(
    live_ref, act_ref, weight_ref, halo_ref, feat_ref, even, odd, wide, tall, left, line
):
    live = live_ref[0].astype(F32)
    tall[...] = halo_ref[...].astype(F32).reshape(512, 128)
    first = tall[pl.ds(0, 32, stride=8), :]
    second = tall[pl.ds(1, 32, stride=8), :]
    line[8:40, :] = second
    line[7:8, :] = tall[4:5, :]
    even[0:32, 0:128] = line[7:39, :].astype(BF)
    even[0:32, 128:256] = first.astype(BF)
    even[0:32, 256:384] = second.astype(BF)
    left[0] = tall[pl.ds(256, 32, stride=8), :]
    left[1] = tall[pl.ds(257, 32, stride=8), :]
    fill_patches(act_ref, even, odd, wide, left)
    result = jnp.dot(even[0:1024, :], weight_ref[0:384, :], preferred_element_type=F32)
    result += jnp.dot(odd[...], weight_ref[384:768, :], preferred_element_type=F32)
    result += jnp.dot(even[32:1056, :], weight_ref[768:1152, :], preferred_element_type=F32)
    feat_ref[...] = (result * live).astype(BF).reshape(32, 32, 256)


def tile_features(live, act, weight_matrix, halo):
    return pl.pallas_call(
        feature_kernel,
        in_specs=[pl.BlockSpec(memory_space=pltpu.SMEM)] + vmem_specs(3),
        out_specs=vmem_specs(1)[0],
        out_shape=jax.ShapeDtypeStruct((32, 32, 256), BF),
        scratch_shapes=[
            pltpu.VMEM((1056, 384), BF),
            pltpu.VMEM((1024, 384), BF),
            pltpu.VMEM((2, 72, 128), F32),
            pltpu.VMEM((512, 128), F32),
            pltpu.VMEM((2, 32, 128), F32),
            pltpu.VMEM((40, 128), F32),
        ],
        cost_estimate=pl.CostEstimate(
            flops=2 * 1024 * 1152 * 256, bytes_accessed=2 << 20, transcendentals=0
        ),
        compiler_params=grant(16),
        name="tile_features",
    )(live, act, weight_matrix, halo)


def gradient_kernel(
    live_ref, cot_ref, weight_ref, halo_ref, grad_ref, wide, tall, shift, around, mix, lines
):
    live = live_ref[0].astype(F32)
    tall[...] = halo_ref[...].astype(F32).reshape(512, 128)

    right = jnp.concatenate(
        [tall[pl.ds(258, 32, stride=8), :], tall[pl.ds(259, 32, stride=8), :]], axis=1
    )
    around[0:32, :] = right
    around[32:33, 0:128] = tall[5:6, :]
    around[32:33, 128:256] = tall[6:7, :]
    below = jnp.concatenate(
        [tall[pl.ds(2, 32, stride=8), :], tall[pl.ds(3, 32, stride=8), :]], axis=1
    )

    def place(i, values):
        shift[0:32, :] = values
        shift[32:33, :] = around[pl.ds(i, 1), :]
        at = pl.ds(pl.multiple_of(i * 32, 32), 32)
        mix[at, 0:256] = values.astype(BF)
        mix[at, 256:512] = shift[1:33, :].astype(BF)

    def one_row(i, carry):
        place(i, cot_ref[i].astype(F32))
        return carry

    lax.fori_loop(0, 32, one_row, 0, unroll=4)
    place(32, below)

    def tap(a, b):
        at = (3 * a + b) * 128
        return weight_ref[at : at + 128, :]

    none = jnp.zeros((128, 256), BF)

    def block(even_taps, odd_taps):
        return jnp.concatenate(
            [jnp.concatenate(even_taps, axis=1), jnp.concatenate(odd_taps, axis=1)], axis=0
        )

    def back(rows, matrix):
        return lax.dot_general(
            rows, matrix, (((1,), (1,)), ((), ())), preferred_element_type=F32
        )

    here, after = mix[0:1024, :], mix[32:1056, :]
    lines[0] = back(here, block([tap(1, 1), none], [tap(1, 2), tap(1, 0)])) * live
    lines[1] = (
        back(here, block([tap(2, 1), none], [tap(2, 2), tap(2, 0)]))
        + back(after, block([tap(0, 1), none], [tap(0, 2), tap(0, 0)]))
    ) * live

    def weave(i, carry):
        at = pl.ds(pl.multiple_of(i * 32, 32), 32)
        for parity in range(2):
            for side in range(2):
                wide[parity, pl.ds(8 + side, 32, stride=2), :] = lines[
                    parity, at, side * 128 : (side + 1) * 128
                ]
            grad_ref[2 * i + parity] = wide[parity, 8:72, :].astype(BF)
        return carry

    lax.fori_loop(0, 32, weave, 0, unroll=4)


def tile_gradient(live, cot, weight_matrix, halo):
    return pl.pallas_call(
        gradient_kernel,
        in_specs=[pl.BlockSpec(memory_space=pltpu.SMEM)] + vmem_specs(3),
        out_specs=vmem_specs(1)[0],
        out_shape=jax.ShapeDtypeStruct((64, 64, 128), BF),
        scratch_shapes=[
            pltpu.VMEM((2, 72, 128), F32),
            pltpu.VMEM((512, 128), F32),
            pltpu.VMEM((40, 256), F32),
            pltpu.VMEM((40, 256), F32),
            pltpu.VMEM((1056, 512), BF),
            pltpu.VMEM((2, 1024, 256), F32),
        ],
        cost_estimate=pl.CostEstimate(
            flops=3 * 1024 * 1152 * 256, bytes_accessed=3 << 20, transcendentals=0
        ),
        compiler_params=grant(20),
        name="tile_gradient",
    )(live, cot, weight_matrix, halo)


def shards(activations, cotangent, weights, tile_list):
    act, cot = activations[0, 0], cotangent[0, 0]
    slots = lax.axis_size("tiles")
    slides = lax.axis_size("slide")
    half_side = cot.shape[0]
    listing = tile_list[0]
    me = lax.axis_index("tiles")
    live = (lax.dynamic_slice_in_dim(listing, me, 1) >= 0).astype(jnp.int32)
    own = lax.axis_index("slide")
    step = jnp.where(me < slots // 2, 1, 3)
    place = jnp.stack([step, me & 1, own, (me >> 1) & 3, live[0]]).astype(jnp.int32)
    select = halo_matrices(listing, me, slots // GW)
    weight_matrix = weights.reshape(-1, weights.shape[3])

    partner = [(t, t ^ 1) for t in range(slots)]
    columns = [[z * 8 + rest for z in range(8)] for rest in range(8)]

    def over_slide(values, hop):
        return lax.ppermute(values, "slide", [(i, (i + hop) % slides) for i in range(slides)])

    def over_x(values, hop):
        pairs = [(t, (t & ~6) | ((((t >> 1) + hop) & 3) << 1)) for t in range(slots)]
        return lax.ppermute(values, "tiles", pairs)

    pieces = lax.all_to_all(pack_edges(act, cot), "tiles", 0, 0, tiled=True)
    keep, send = interior_weights(place, act, cot)
    got = lax.ppermute(send, "tiles", partner)
    edges, send_edges = edge_weights(place, pieces, select)
    back = turn_edges(pieces, select)

    got_edges = lax.ppermute(send_edges, "tiles", partner)
    quarters = join_and_cut(place, keep, got, edges, got_edges)
    moved = []
    for hop in range(1, 4):
        moved.append(over_slide(quarters[hop], hop))
    halo = lax.all_to_all(back, "tiles", 0, 0, tiled=True)
    cuts = sum_and_cut(place, 3, [quarters[0]] + moved)
    moved = []
    for hop in range(1, 4):
        moved.append(over_x(cuts[hop], hop))
    copies = sum_and_copy([cuts[0]] + moved, 8)
    copies, halo = lax.optimization_barrier((copies, halo))
    parts = lax.all_to_all(copies, "tiles", 0, 0, tiled=True, axis_index_groups=columns)
    grad_scale = 1.0 / math.sqrt(slides * slots * half_side * half_side)
    eighth = sum_scaled(parts, grad_scale)

    features_out = tile_features(live, act, weight_matrix, halo)
    input_grad = tile_gradient(live, cot, weight_matrix, halo)

    eighths = [eighth]
    for hop in range(1, 4):
        eighths.append(over_x(eighth, hop))
    quarter = assemble(place, 3, eighths)
    mine = [quarter]
    for hop in range(1, 4):
        mine.append(over_slide(quarter, hop))
    theirs = []
    for hop in range(4):
        theirs.append(lax.ppermute(mine[hop], "tiles", partner))
    weight_grad = final_weights(place, mine, theirs).reshape(weights.shape)
    return (features_out[None, None], input_grad[None, None], weight_grad)


def solution(mesh):
    placed = (
        P("slide", "tiles", None, None, None),
        P("slide", "tiles", None, None, None),
        P(),
        P("slide", None),
    )
    return jax.shard_map(
        shards,
        mesh=mesh,
        in_specs=placed,
        out_specs=(
            P("slide", "tiles", None, None, None),
            P("slide", "tiles", None, None, None),
            P(),
        ),
        check_vma=False,
    )
```
